256 devices in a mesh: section: 2 (over z_lo), owner: 32 (over x, z_hi, core), context: 4 (over y).
Axes of the slice: x: 4, y: 4, z: 8 (z_hi: 4, z_lo: 2; z = z_hi * 2 + z_lo), core: 2. Of those that a mesh axis runs over, the one named last changes fastest.
Arguments:
- x_attn: bfloat16 [16384, 8192], P(('section', 'context'), 'owner'), parts along dimension 0, may hold values from -6 to 6
- x_mlp: bfloat16 [16384, 8192], P(('section', 'context'), 'owner'), parts along dimension 0, may hold values from -6 to 6
- x_down: bfloat16 [16384, 29568], P(('section', 'context'), 'owner'), parts along dimension 0, may hold values from -6 to 6
- omega_attn: bfloat16 [16384, 256], P(('section', 'owner')), parts along dimension 0, may hold values from -6 to 6
- omega_mlp: bfloat16 [16384, 256], P(('section', 'owner')), parts along dimension 0, may hold values from -6 to 6
- omega_down: bfloat16 [59136, 256], P(('section', 'owner')), parts along dimension 0, may hold values from -6 to 6
- basis_attn: bfloat16 [16384, 256], P(('section', 'owner')), parts along dimension 0, may hold values from -1 to 1
- basis_mlp: bfloat16 [16384, 256], P(('section', 'owner')), parts along dimension 0, may hold values from -1 to 1
- basis_down: bfloat16 [59136, 256], P(('section', 'owner')), parts along dimension 0, may hold values from -1 to 1
- eig_attn: float32 [512], P('section'), parts along dimension 0, may hold values from 2 to 20
- eig_mlp: float32 [512], P('section'), parts along dimension 0, may hold values from 2 to 20
- eig_down: float32 [512], P('section'), parts along dimension 0, may hold values from 2 to 20
Outputs:
- sketch_attn: float32 [16384, 256], P(('section', 'owner', 'context')), parts along dimension 0
- sketch_mlp: float32 [16384, 256], P(('section', 'owner', 'context')), parts along dimension 0
- sketch_down: float32 [59136, 256], P(('section', 'owner', 'context')), parts along dimension 0
The draws below stay inside these ranges and needn't reach their ends.
There are 2 independent parts, one for each index of `section`. The reference program is written for one: setup_inputs(seed, part) draws one part's arguments, and reference() takes and returns one part's arrays. A program takes and returns all parts, laid end to end along the dimension named above; each array names one. Nothing has to cross between parts.
All inputs are finite; a program needn't handle non-finite values.
Results may differ from the reference program's by a relative error of at most 0.0003.
Values may be sent and summed in bfloat16 or wider, within the bound.
A program may use at most 64 MiB of HBM per device.

```python
import math
import jax
import jax.numpy as jnp
from jax import lax

D = 8192
FF = 29568
R = 256
TOKENS = 8192


def drawn_draw(key, label, rows, cols, scale):
    own_key = jax.random.fold_in(key, label)
    values = jnp.clip(jax.random.normal(jax.random.fold_in(own_key, 13), (rows, cols), jnp.float32), -6.0, 6.0)
    return (values * scale).astype(jnp.bfloat16)


def draw_x_attn(key, part):
    return drawn_draw(key, 1, TOKENS, D, 1.0)


def draw_x_mlp(key, part):
    return drawn_draw(key, 2, TOKENS, D, 1.0)


def draw_x_down(key, part):
    return drawn_draw(key, 3, TOKENS, FF, 1.0)


def draw_omega_attn(key, part):
    return drawn_draw(key, 4, D, R, 1.0)


def draw_omega_mlp(key, part):
    return drawn_draw(key, 5, D, R, 1.0)


def draw_omega_down(key, part):
    return drawn_draw(key, 6, FF, R, 1.0)


def draw_basis_attn(key, part):
    return drawn_draw(key, 7, D, R, 1.0 / D ** 0.5)


def draw_basis_mlp(key, part):
    return drawn_draw(key, 8, D, R, 1.0 / D ** 0.5)


def draw_basis_down(key, part):
    return drawn_draw(key, 9, FF, R, 1.0 / FF ** 0.5)


def setup_inputs(seed: int = 0, part: int = 0) -> dict:
    arg_keys = jax.random.split(jax.random.key(seed), 13)
    own_keys = jax.random.split(jax.random.fold_in(arg_keys[12], part), 13)
    x_attn = draw_x_attn(jax.random.fold_in(jax.random.fold_in(arg_keys[12], part), 71), part)
    x_mlp = draw_x_mlp(jax.random.fold_in(jax.random.fold_in(arg_keys[12], part), 71), part)
    x_down = draw_x_down(jax.random.fold_in(jax.random.fold_in(arg_keys[12], part), 71), part)
    omega_attn = draw_omega_attn(jax.random.fold_in(jax.random.fold_in(arg_keys[12], part), 71), part)
    omega_mlp = draw_omega_mlp(jax.random.fold_in(jax.random.fold_in(arg_keys[12], part), 71), part)
    omega_down = draw_omega_down(jax.random.fold_in(jax.random.fold_in(arg_keys[12], part), 71), part)
    basis_attn = draw_basis_attn(jax.random.fold_in(jax.random.fold_in(arg_keys[12], part), 71), part)
    basis_mlp = draw_basis_mlp(jax.random.fold_in(jax.random.fold_in(arg_keys[12], part), 71), part)
    basis_down = draw_basis_down(jax.random.fold_in(jax.random.fold_in(arg_keys[12], part), 71), part)
    eig_attn = jnp.clip(jnp.exp(jax.random.uniform(own_keys[9], (R,), jnp.float32, math.log(2.0), math.log(20.0))), 2.0, 20.0)
    eig_mlp = jnp.clip(jnp.exp(jax.random.uniform(own_keys[10], (R,), jnp.float32, math.log(2.0), math.log(20.0))), 2.0, 20.0)
    eig_down = jnp.clip(jnp.exp(jax.random.uniform(own_keys[11], (R,), jnp.float32, math.log(2.0), math.log(20.0))), 2.0, 20.0)
    return {"x_attn": x_attn, "x_mlp": x_mlp, "x_down": x_down, "omega_attn": omega_attn, "omega_mlp": omega_mlp, "omega_down": omega_down, "basis_attn": basis_attn, "basis_mlp": basis_mlp, "basis_down": basis_down, "eig_attn": eig_attn, "eig_mlp": eig_mlp, "eig_down": eig_down}


def one_factor(inputs, omega, basis, eigen, total):
    probe = jnp.dot(inputs, omega, preferred_element_type=jnp.float32).astype(jnp.bfloat16)
    core = jnp.dot(basis.T, omega, preferred_element_type=jnp.float32)
    data = jnp.dot(inputs.T, probe, preferred_element_type=jnp.float32)
    weighted = eigen[:, None] * core
    prior = jnp.dot(basis.astype(jnp.float32), weighted, precision=lax.Precision.HIGHEST)
    return 0.9 * prior + (0.1 / total) * data


def reference(x_attn, x_mlp, x_down, omega_attn, omega_mlp, omega_down, basis_attn, basis_mlp, basis_down, eig_attn, eig_mlp, eig_down):
    total = x_attn.shape[0]
    first = one_factor(x_attn, omega_attn, basis_attn, eig_attn, total)
    second = one_factor(x_mlp, omega_mlp, basis_mlp, eig_mlp, total)
    third = one_factor(x_down, omega_down, basis_down, eig_down, total)
    return (first, second, third)
```

```python
import jax
import jax.numpy as jnp
from jax import lax
from jax.experimental import pallas as pl
from jax.experimental.pallas import tpu as pltpu
from jax.sharding import PartitionSpec as P

ORDER = (2, 0, 1)
SEMS = 40


def halves(rows, unit):
    a = -(-(rows // 2) // unit) * unit
    return a, rows - a


def sketch_kernel(total, tokens, turned, *refs):
    xs, ws, bs, es, outs = refs[0:3], refs[3:6], refs[6:9], refs[9:12], refs[12:15]
    s = refs[15]
    ssem, rsem, lsem = s["ssem"], s["rsem"], s["lsem"]
    owner, ctx = lax.axis_index("owner"), lax.axis_index("context")
    core, zi, xi = lax.rem(owner, 2), lax.rem(lax.div(owner, 2), 4), lax.div(owner, 8)

    def at(x, z, c):
        return {"owner": (lax.rem(x, 4) * 4 + lax.rem(z, 4)) * 2 + c}

    partner = at(xi, zi, 1 - core)
    xp, xm = at(xi + 1, zi, core), at(xi + 3, zi, core)
    zp, zm = at(xi, zi + 1, core), at(xi, zi + 3, core)
    yp, ym = {"context": lax.rem(ctx + 1, 4)}, {"context": lax.rem(ctx + 3, 4)}

    pending = []

    def remote(i, src, dst, dev):
        return pltpu.make_async_remote_copy(
            src_ref=src, dst_ref=dst, send_sem=ssem.at[i], recv_sem=rsem.at[i],
            device_id=dev, device_id_type=pl.DeviceIdType.MESH,
        )

    def send(i, src, dst, dev):
        copy = remote(i, src, dst, dev)
        copy.start()
        pending.append(copy)

    def recv(i, dst, dev):
        remote(i, dst, dst, dev).wait_recv()

    half = tokens // 2
    xv, wv, bv, ev = s["xv"], s["wv"], s["bv"], s["ev"]
    loads = {}
    for f in ORDER:
        loads["w", f] = pltpu.make_async_copy(ws[f], wv[f], lsem.at[f])
        for q, c in enumerate((1 - core, core)):
            rows = pl.ds(pl.multiple_of(c * half, half), half)
            where = (slice(None), rows) if turned[f] else rows
            loads["x", f, q] = pltpu.make_async_copy(
                xs[f].at[where], xv[f].at[where], lsem.at[3 + 2 * f + q])
        loads["b", f] = pltpu.make_async_copy(bs[f], bv[f], lsem.at[9 + f])
        loads["e", f] = pltpu.make_async_copy(es[f], ev[f], lsem.at[12 + f])
    for f in ORDER:
        for part in (("w", f), ("x", f, 0), ("x", f, 1)):
            loads[part].start()
    for f in ORDER:
        for part in (("b", f), ("e", f)):
            loads[part].start()

    barrier = pltpu.get_barrier_semaphore()
    for dev in (partner, xp, xm, zp, zm, yp, ym):
        pl.semaphore_signal(barrier, inc=1, device_id=dev, device_id_type=pl.DeviceIdType.MESH)
    pl.semaphore_wait(barrier, 7)

    def around(i):
        return lax.rem(i + 2, 4), lax.rem(i + 1, 4), lax.rem(i + 3, 4), i

    def rs_start(blocks, r1, r2, a, b, idx, devs, sem, pre):
        i2, ip, im, me = around(idx)
        plus, minus = devs
        pre(i2, 0)
        send(sem, blocks.at[i2, 0:a], r1.at[0, 0:a], plus)
        if b:
            send(sem + 1, blocks.at[i2, a:a + b], r1.at[1, 0:b], minus)
        pre(ip, 1)
        if b:
            send(sem + 2, blocks.at[ip, a:a + b], r2.at[0, a:a + b], plus)
        pre(im, 2)
        send(sem + 3, blocks.at[im, 0:a], r2.at[1, 0:a], minus)
        pre(me, 3)

    def rs_mid(blocks, r1, r2, a, b, idx, devs, sem):
        i2, ip, im, me = around(idx)
        plus, minus = devs
        recv(sem, r1.at[0, 0:a], plus)
        blocks[ip, 0:a] = blocks[ip, 0:a] + r1[0, 0:a]
        send(sem + 4, blocks.at[ip, 0:a], r2.at[0, 0:a], plus)
        if b:
            recv(sem + 1, r1.at[1, 0:b], minus)
            blocks[im, a:a + b] = blocks[im, a:a + b] + r1[1, 0:b]
            send(sem + 5, blocks.at[im, a:a + b], r2.at[1, a:a + b], minus)

    def rs_end(r2, a, b, devs, sem):
        plus, minus = devs
        recv(sem + 3, r2.at[1, 0:a], minus)
        recv(sem + 4, r2.at[0, 0:a], plus)
        if b:
            recv(sem + 2, r2.at[0, a:a + b], plus)
            recv(sem + 5, r2.at[1, a:a + b], minus)

    def ag_start(block, idx, devs, sem):
        for q, dev in enumerate(devs):
            send(sem + q, block(idx), block(idx), dev)

    def ag_mid(block, part, two, idx, devs, sem, got=None):
        i2, ip, im, me = around(idx)
        plus, minus = devs
        recv(sem, block(im), plus)
        send(sem + 2, part(im, 0), part(im, 0), plus)
        if got:
            got(im, 1)
        recv(sem + 1, block(ip), minus)
        if two:
            send(sem + 3, part(ip, 1), part(ip, 1), minus)
        if got:
            got(ip, 2)

    def ag_end(part, two, idx, devs, sem):
        i2 = around(idx)[0]
        recv(sem + 2, part(i2, 0), devs[0])
        if two:
            recv(sem + 3, part(i2, 1), devs[1])

    xdev, zdev, ydev = (xp, xm), (zp, zm), (yp, ym)

    class Chunk:
        pass

    chunks = []
    for k, c in enumerate(s["chunks"]):
        ch = Chunk()
        ch.k, ch.sem = k, k * SEMS
        for name, ref in c.items():
            setattr(ch, name, ref)
        ch.xb, ch.zb = ch.own.shape[1], ch.g.shape[3]
        unit = 8 if k == 0 else 16
        ch.xa, ch.xc = halves(ch.xb, unit)
        ch.za, ch.zc = halves(ch.zb, unit)
        ch.f = None if k == 0 else ORDER[k - 1]
        chunks.append(ch)

    waited = set()

    def load_wait(*part):
        if part not in waited:
            waited.add(part)
            loads[part].wait()

    rows_c = bv[0].shape[1] // 4
    mine = pl.ds(pl.multiple_of(ctx * rows_c, rows_c), rows_c)

    def stage_core():
        ch = chunks[0]
        for f in ORDER:
            load_wait("w", f)
            load_wait("b", f)
            s["cfull"][f] = lax.dot_general(
                bv[f][...], wv[f][...], (((0,), (0,)), ((), ())), preferred_element_type=jnp.float32)
        part = s["cpart"]
        for f in range(3):
            part[f // 2, (f % 2) * 2:(f % 2) * 2 + 2] = s["cfull"][f, mine].reshape(2, ch.xb, -1)
        part[1, 2:4] = jnp.zeros_like(part[1, 2:4])
        for q, i in enumerate(around(xi)):
            send(ch.sem + q, part.at[1 - core, i], ch.cr.at[i], partner)
        for i in range(4):
            ch.own[i] = part[core, i]

    def tile_probe(f, row, dst):
        rows = dst.shape[0]
        where = pl.ds(pl.multiple_of(row, rows), rows)
        if turned[f]:
            dst[...] = lax.dot_general(
                xv[f][:, where], wv[f][...], (((0,), (0,)), ((), ())),
                preferred_element_type=jnp.float32)
        else:
            dst[...] = jnp.dot(xv[f][where], wv[f][...], preferred_element_type=jnp.float32)

    def stage_probe(ch):
        load_wait("w", ch.f)
        load_wait("x", ch.f, 0)
        for q, i in enumerate(around(xi)):
            tile_probe(ch.f, (1 - core) * half + i * ch.xb, ch.cs.at[i])
            send(ch.sem + q, ch.cs.at[i], ch.cr.at[i], partner)
        load_wait("x", ch.f, 1)
        for i in around(xi):
            tile_probe(ch.f, core * half + i * ch.xb, ch.own.at[i])

    def stage_a(ch):
        def pre(i, q):
            recv(ch.sem + q, ch.cr.at[i], partner)
            ch.own[i] = ch.own[i] + ch.cr[i]
        rs_start(ch.own, ch.xr1, ch.xr2, ch.xa, ch.xc, xi, xdev, ch.sem + 4, pre)

    def stage_b(ch):
        rs_mid(ch.own, ch.xr1, ch.xr2, ch.xa, ch.xc, xi, xdev, ch.sem + 4)

    def stage_d(ch):
        rs_end(ch.xr2, ch.xa, ch.xc, xdev, ch.sem + 4)

        def pre(i, q):
            rows = pl.ds(pl.multiple_of(i * ch.zb, ch.zb), ch.zb)
            ch.zs[i] = ch.own[xi, rows] + ch.xr2[0, rows] + ch.xr2[1, rows]
        rs_start(ch.zs, ch.zr1, ch.zr2, ch.za, ch.zc, zi, zdev, ch.sem + 10, pre)

    def stage_e(ch):
        rs_mid(ch.zs, ch.zr1, ch.zr2, ch.za, ch.zc, zi, zdev, ch.sem + 10)

    def zblock(ch):
        return lambda i: ch.g.at[core, xi, i]

    def zpart(ch):
        return lambda i, h: ch.g.at[core, xi, i, (0 if h == 0 else ch.za):(ch.za if h == 0 else ch.zb)]

    def xblock(ch):
        return lambda i: ch.g.at[core, i]

    def xpart(ch):
        return lambda i, h: ch.g.at[core, i, 2 * h:2 * h + 2]

    def stage_f(ch):
        rs_end(ch.zr2, ch.za, ch.zc, zdev, ch.sem + 10)
        ch.g[core, xi, zi] = (ch.zs[zi] + ch.zr2[0] + ch.zr2[1]).astype(ch.g.dtype)
        ag_start(zblock(ch), zi, zdev, ch.sem + 16)

    def stage_g(ch):
        ag_mid(zblock(ch), zpart(ch), ch.zc > 0, zi, zdev, ch.sem + 16)

    def forward(ch):
        def got(i, q):
            send(ch.sem + 24 + q, ch.g.at[core, i], ch.g.at[core, i], partner)
        return got

    def stage_h(ch):
        ag_end(zpart(ch), ch.zc > 0, zi, zdev, ch.sem + 16)
        ag_start(xblock(ch), xi, xdev, ch.sem + 20)
        forward(ch)(xi, 0)

    def stage_i(ch):
        ag_mid(xblock(ch), xpart(ch), True, xi, xdev, ch.sem + 20, forward(ch))

    def stage_j(ch):
        ag_end(xpart(ch), True, xi, xdev, ch.sem + 20)
        i2, ip, im, me = around(xi)
        forward(ch)(i2, 3)
        for q, i in enumerate((me, im, ip, i2)):
            recv(ch.sem + 24 + q, ch.g.at[1 - core, i], partner)

    def stage_prior():
        g = chunks[0].g
        for f in ORDER:
            load_wait("e", f)
            pair = g[f // 2, (f % 2) * 2:(f % 2) * 2 + 2].reshape(rows_c, -1)
            row = lax.broadcasted_iota(jnp.int32, pair.shape, 0) + ctx * rows_c
            col = lax.broadcasted_iota(jnp.int32, pair.shape, 1)
            eig = jnp.sum(jnp.where(row == col, ev[f][...], 0.0), axis=1, keepdims=True)
            weighted = pair * (0.9 * eig)
            high = weighted.astype(jnp.bfloat16)
            low = (weighted - high.astype(jnp.float32)).astype(jnp.bfloat16)
            wp = s["wp"]
            wp[0] = jnp.zeros_like(wp[0])
            wp[1] = jnp.zeros_like(wp[1])
            wp[0, mine] = high
            wp[1, mine] = low
            d = s["d"][f]
            rows = d.shape[0]
            for r in range(0, rows, 256):
                n = min(256, rows - r)
                b = bv[f][r:r + n]
                d[r:r + n] = (jnp.dot(b, wp[0], preferred_element_type=jnp.float32)
                              + jnp.dot(b, wp[1], preferred_element_type=jnp.float32))

    def stage_t(f):
        if turned[f]:
            return
        rows = xv[f].shape[1]

        @pl.loop(0, tokens // 256)
        def _(t):
            cols = pl.ds(pl.multiple_of(t * 256, 256), 256)
            for r in range(0, rows, 256):
                n = min(256, rows - r)
                s["xt"][f][r:r + n, cols] = xv[f][cols, r:r + n].T

    def stage_k(ch):
        f, d = ch.f, s["d"][ch.f]
        z = ch.g[...].reshape(tokens, -1)
        xt = xv[f] if turned[f] else s["xt"][f]
        rows = d.shape[0]
        for r in range(0, rows, 256):
            n = min(256, rows - r)
            d[r:r + n] = d[r:r + n] + (0.1 / total) * jnp.dot(
                xt[r:r + n], z, preferred_element_type=jnp.float32)
        dp, fb = s["dp"][f], rows // 4
        for i in range(4):
            dp[i, 0:fb] = d[i * fb:(i + 1) * fb]
        n = dp.shape[1]
        ch.ya, ch.yc = halves(n, 8)
        rs_start(dp, s["yr1"][f], s["yr2"][f], ch.ya, ch.yc, ctx, ydev, ch.sem + 28, lambda i, q: None)

    def stage_l(ch):
        f = ch.f
        rs_mid(s["dp"][f], s["yr1"][f], s["yr2"][f], ch.ya, ch.yc, ctx, ydev, ch.sem + 28)

    def stage_m(ch):
        f = ch.f
        rs_end(s["yr2"][f], ch.ya, ch.yc, ydev, ch.sem + 28)
        n = outs[f].shape[0]
        r2 = s["yr2"][f]
        outs[f][...] = s["dp"][f][ctx, 0:n] + r2[0, 0:n] + r2[1, 0:n]

    for f in range(3):
        dp = s["dp"][f]
        n = outs[f].shape[0]
        if dp.shape[1] != n:
            dp[...] = jnp.zeros_like(dp)

    c0, c1, c2, c3 = chunks
    events = [
        (0.0, lambda: stage_probe(c1)), (3.0, lambda: stage_a(c1)),
        (3.1, stage_core), (3.2, lambda: stage_probe(c2)), (3.3, lambda: stage_a(c0)),
        (3.4, lambda: stage_probe(c3)), (40.0, None),
    ]
    times = {"b": 4.5, "d": 10, "e": 13, "f": 16, "g": 18.5, "h": 21, "i": 27, "j": 30, "k": 30.1,
             "l": 33.5, "m": 37}
    stages = {"b": stage_b, "d": stage_d, "e": stage_e, "f": stage_f, "g": stage_g, "h": stage_h,
              "i": stage_i, "j": stage_j, "k": stage_k, "l": stage_l, "m": stage_m}
    for ch, t0 in ((c0, 5.0), (c1, 3.0), (c2, 9.0), (c3, 17.0)):
        if ch.k >= 2:
            events.append((t0 - 0.4, lambda ch=ch: stage_a(ch)))
        for name, t in times.items():
            if ch.k == 0 and name in "klm":
                continue
            events.append((t0 + t, lambda ch=ch, name=name: stages[name](ch)))
    events.append((8.7, lambda: stage_t(ORDER[0])))
    events.append((17.2, lambda: stage_t(ORDER[1])))
    events.append((17.3, lambda: stage_t(ORDER[2])))
    events = [e for e in events if e[1] is not None]
    prior_at = max(5.0 + times["j"], 0) + 0.01
    down_k = 3.0 + times["k"]
    events = [(t, fn) for t, fn in events]
    events.append((min(prior_at, 1e9), stage_prior))
    events = [(t + (prior_at - down_k + 0.02 if prior_at > down_k and t >= down_k and t < prior_at
                    and fn is not stage_prior and t == down_k else 0), fn) for t, fn in events]
    for _, fn in sorted(events, key=lambda e: e[0]):
        fn()

    for copy in pending:
        copy.wait_send()


def sketch(total, xs, ws, bs, es):
    tokens = xs[0].shape[0]
    r = ws[0].shape[1]
    f32, bf16 = jnp.float32, jnp.bfloat16
    vm = pltpu.VMEM

    def chunk(h, dtype, first):
        xb, zb = h // 4, h // 16
        unit = 8 if first else 16
        xa, za = halves(xb, unit)[0], halves(zb, unit)[0]
        c = dict(
            own=vm((4, xb, r), f32), cr=vm((4, xb, r), f32), zs=vm((4, zb, r), f32),
            xr1=vm((2, xa, r), f32), xr2=vm((2, xb, r), f32),
            zr1=vm((2, za, r), f32), zr2=vm((2, zb, r), f32), g=vm((2, 4, 4, zb, r), dtype),
        )
        if not first:
            c["cs"] = vm((4, xb, r), f32)
        return c

    fs = [x.shape[1] for x in xs]
    turned = [f % 128 != 0 for f in fs]
    xs = [x.T if turn else x for x, turn in zip(xs, turned)]
    fb = [-(-(f // 4) // 8) * 8 for f in fs]
    scratch = dict(
        chunks=[chunk(r // 2, f32, True)] + [chunk(tokens // 2, bf16, False) for _ in range(3)],
        xv=[vm(x.shape, bf16) for x in xs], wv=[vm((f, r), bf16) for f in fs],
        bv=[vm((f, r), bf16) for f in fs], ev=[vm((1, r), f32) for f in fs],
        xt=[vm((8, 128) if turn else (f, tokens), bf16) for f, turn in zip(fs, turned)], d=[vm((f, r), f32) for f in fs],
        dp=[vm((4, n, r), f32) for n in fb], yr1=[vm((2, halves(n, 8)[0], r), f32) for n in fb],
        yr2=[vm((2, n, r), f32) for n in fb],
        cfull=vm((3, r, r), f32), cpart=vm((2, 4, r // 8, r), f32), wp=vm((2, r, r), bf16),
        ssem=pltpu.SemaphoreType.DMA((4 * SEMS,)), rsem=pltpu.SemaphoreType.DMA((4 * SEMS,)),
        lsem=pltpu.SemaphoreType.DMA((15,)),
    )

    def body(*refs):
        sketch_kernel(total, tokens, turned, *refs)

    return pl.pallas_call(
        body,
        out_shape=[jax.ShapeDtypeStruct((f // 4, r), f32) for f in fs],
        in_specs=[pl.BlockSpec(memory_space=pl.ANY)] * 12,
        out_specs=[pl.BlockSpec(memory_space=pltpu.VMEM)] * 3,
        scratch_shapes=(scratch,),
        compiler_params=pltpu.CompilerParams(
            collective_id=0, has_side_effects=True, vmem_limit_bytes=60 * 2**20),
        name="sketch",
    )(*xs, *ws, *bs, *[e.reshape(1, r) for e in es])


def solution(mesh):
    def per_device(*args):
        total = args[0].shape[0] * mesh.shape["context"]
        return tuple(sketch(total, args[0:3], args[3:6], args[6:9], args[9:12]))

    rows = P(("section", "owner"), None)
    return jax.shard_map(
        per_device,
        mesh=mesh,
        in_specs=(P(("section", "context"), "owner"),) * 3 + (rows,) * 6 + (P("section"),) * 3,
        out_specs=(P(("section", "owner", "context"), None),) * 3,
        check_vma=False,
    )
```

```python
import jax
import jax.numpy as jnp
from jax import lax
from jax.experimental import pallas as pl
from jax.experimental.pallas import tpu as pltpu
from jax.sharding import PartitionSpec as P

PLAN = ((2, 2), (0, 2), (1, 2))
SEMS = 32
SCHEDULE = [
    "p1", "p0", "p2", "a0", "a1", "p3", "p4", "a2", "p5", "a3", "p6", "a4", "t0", "a5",
    "d0", "t1", "a6", "d1", "d2", "d3", "f0", "d4", "f1", "d5", "f2", "d6", "f3", "h0",
    "f4", "h1", "i0", "f5", "h2", "j0", "w0", "f6", "i1", "h3", "h4", "j1", "k1", "i2",
    "h5", "j2", "k2", "i3", "h6", "i4", "j3", "k3", "j4", "i5", "k4", "j5", "k5", "i6",
    "j6", "k6",
]
SPAN = 86.0
SCALE_ROWS = 16


def encode(src, dst):
    rows = src.shape[0]
    tiles = [(r, min(r + 64, rows)) for r in range(0, rows, 64)]
    top = None
    for lo, hi in tiles:
        peak = jnp.max(jnp.abs(src[lo:hi]), axis=0, keepdims=True)
        top = peak if top is None else jnp.maximum(top, peak)
    scale = (top * 1.01 + 1e-30).astype(jnp.bfloat16)
    base = dst.shape[0] - SCALE_ROWS
    dst[base:base + SCALE_ROWS] = jnp.broadcast_to(scale, (SCALE_ROWS, src.shape[1]))
    slope = (2.0 * SPAN) / dst[base:base + SCALE_ROWS].astype(jnp.float32)[0:1]
    for lo, hi in tiles:
        v = src[lo:hi]
        y = jnp.exp(jnp.abs(v) * slope - SPAN)
        dst[lo:hi] = jnp.where(v < 0, -y, y).astype(jnp.bfloat16)


def decode(src, r, n):
    base = src.shape[0] - SCALE_ROWS
    slope = src[base:base + SCALE_ROWS].astype(jnp.float32)[0:1] * (0.5 / SPAN)
    y = src[pl.ds(r, n)].astype(jnp.float32)
    v = (jnp.log(jnp.abs(y)) + SPAN) * slope
    return jnp.where(y < 0, -v, v)


def sketch_kernel(total, tokens, turned, *refs):
    xs, ws, bs, es, outs = refs[0:3], refs[3:6], refs[6:9], refs[9:12], refs[12:15]
    s = refs[15]
    ssem, rsem, lsem = s["ssem"], s["rsem"], s["lsem"]
    owner, ctx = lax.axis_index("owner"), lax.axis_index("context")
    core, zi, xi = lax.rem(owner, 2), lax.rem(lax.div(owner, 2), 4), lax.div(owner, 8)

    def at(x, z, c):
        return {"owner": (lax.rem(x, 4) * 4 + lax.rem(z, 4)) * 2 + c}

    partner = at(xi, zi, 1 - core)
    hops = (2, 1, 3)
    xdev = [at(xi + h, zi, core) for h in hops]
    zdev = [at(xi, zi + h, core) for h in hops]
    ydev = [{"context": lax.rem(ctx + h, 4)} for h in hops]

    pending = []

    def remote(i, src, dst, dev):
        return pltpu.make_async_remote_copy(
            src_ref=src, dst_ref=dst, send_sem=ssem.at[i], recv_sem=rsem.at[i],
            device_id=dev, device_id_type=pl.DeviceIdType.MESH,
        )

    def send(i, src, dst, dev):
        copy = remote(i, src, dst, dev)
        copy.start()
        pending.append(copy)

    def recv(i, dst, dev):
        remote(i, dst, dst, dev).wait_recv()

    half = tokens // 2
    xv, wv, bv, ev = s["xv"], s["wv"], s["bv"], s["ev"]
    factors = [f for f, _ in PLAN]
    loads = {}
    for f in factors:
        loads["w", f] = pltpu.make_async_copy(ws[f], wv[f], lsem.at[f])
        for q, c in enumerate((1 - core, core)):
            rows = pl.ds(pl.multiple_of(c * half, half), half)
            where = (slice(None), rows) if turned[f] else rows
            loads["x", f, q] = pltpu.make_async_copy(
                xs[f].at[where], xv[f].at[where], lsem.at[3 + 2 * f + q])
        loads["b", f] = pltpu.make_async_copy(bs[f], bv[f], lsem.at[9 + f])
        loads["e", f] = pltpu.make_async_copy(es[f], ev[f], lsem.at[12 + f])
    first = factors[0]
    order = [("w", first), ("x", first, 0), ("x", first, 1)]
    order += [("w", f) for f in factors[1:]] + [("b", f) for f in factors]
    order += [("x", f, q) for f in factors[1:] for q in (0, 1)] + [("e", f) for f in factors]
    for part in order:
        loads[part].start()

    barrier = pltpu.get_barrier_semaphore()
    peers = [partner] + xdev + zdev + ydev
    for dev in peers:
        pl.semaphore_signal(barrier, inc=1, device_id=dev, device_id_type=pl.DeviceIdType.MESH)

    waited = set()

    def load_wait(*part):
        if part not in waited:
            waited.add(part)
            loads[part].wait()

    def around(i):
        return [lax.rem(i + h, 4) for h in hops]

    class Chunk:
        pass

    chunks = []
    for k, c in enumerate(s["chunks"]):
        ch = Chunk()
        ch.k, ch.sem = k, k * SEMS
        for name, ref in c.items():
            setattr(ch, name, ref)
        ch.xb, ch.zb = ch.own.shape[1], ch.g.shape[3]
        chunks.append(ch)
    k = 1
    for f, pieces in PLAN:
        for piece in range(pieces):
            chunks[k].f, chunks[k].t0, chunks[k].last = f, piece * (half // pieces), piece == pieces - 1
            k += 1

    rows_c = bv[0].shape[1] // 4
    mine = pl.ds(pl.multiple_of(ctx * rows_c, rows_c), rows_c)

    def stage_core():
        ch = chunks[0]
        part = s["cpart"]
        for f in factors:
            load_wait("w", f)
            load_wait("b", f)
            s["cfull"][...] = lax.dot_general(
                bv[f][...], wv[f][...], (((0,), (0,)), ((), ())), preferred_element_type=jnp.float32)
            part[f // 2, (f % 2) * 2:(f % 2) * 2 + 2] = s["cfull"][mine].reshape(2, ch.xb, -1)
        part[1, 2:4] = jnp.zeros_like(part[1, 2:4])
        for q, i in enumerate(around(xi) + [xi]):
            send(ch.sem + q, part.at[1 - core, i], ch.cr.at[i], partner)
        for i in range(4):
            ch.own[i] = part[core, i]

    def tile_probe(f, row, dst):
        rows = dst.shape[0]
        where = pl.ds(pl.multiple_of(row, rows), rows)
        if turned[f]:
            dst[...] = lax.dot_general(
                xv[f][:, where], wv[f][...], (((0,), (0,)), ((), ())),
                preferred_element_type=jnp.float32)
        else:
            dst[...] = jnp.dot(xv[f][where], wv[f][...], preferred_element_type=jnp.float32)

    def stage_probe(ch, after_first=None):
        load_wait("w", ch.f)
        load_wait("x", ch.f, 0)
        for q, i in enumerate(around(xi) + [xi]):
            tile_probe(ch.f, (1 - core) * half + ch.t0 + i * ch.xb, ch.cs.at[i])
            if q == 0 and after_first:
                after_first()
            send(ch.sem + q, ch.cs.at[i], ch.cr.at[i], partner)
        load_wait("x", ch.f, 1)
        for i in around(xi) + [xi]:
            tile_probe(ch.f, core * half + ch.t0 + i * ch.xb, ch.own.at[i])

    def stage_a(ch):
        for q, i in enumerate(around(xi) + [xi]):
            recv(ch.sem + q, ch.cr.at[i], partner)
            ch.own[i] = ch.own[i] + ch.cr[i]
            if q < 3:
                if ch.k == 0:
                    send(ch.sem + 4 + q, ch.own.at[i], ch.xr.at[q], xdev[q])
                else:
                    encode(ch.own.at[i], ch.xs.at[q])
                    send(ch.sem + 4 + q, ch.xs.at[q], ch.xr.at[q], xdev[q])

    def stage_d(ch):
        for q in (1, 2, 0):
            recv(ch.sem + 4 + q, ch.xr.at[q], xdev[q])
        for q, i in enumerate(around(zi) + [zi]):
            r = pl.multiple_of(i * ch.zb, ch.zb)
            rows = pl.ds(r, ch.zb)
            v = ch.own[xi, rows]
            for p in range(3):
                v = v + (ch.xr[p, rows] if ch.k == 0 else decode(ch.xr.at[p], r, ch.zb))
            ch.zs[i] = v
            if q < 3 and ch.k == 0:
                send(ch.sem + 7 + q, ch.zs.at[i], ch.zr.at[q], zdev[q])
            elif q < 3:
                encode(ch.zs.at[i], ch.zx.at[q])
                send(ch.sem + 7 + q, ch.zx.at[q], ch.zr.at[q], zdev[q])

    def stage_f(ch):
        for q in (1, 2, 0):
            recv(ch.sem + 7 + q, ch.zr.at[q], zdev[q])
        v = ch.zs[zi]
        for p in range(3):
            v = v + (ch.zr[p] if ch.k == 0 else decode(ch.zr.at[p], 0, ch.zb))
        ch.g[core, xi, zi] = v.astype(ch.g.dtype)
        for q in range(3):
            block = ch.g.at[core, xi, zi]
            send(ch.sem + 10 + q, block, block, zdev[q])

    def source(i, q):
        return lax.rem(i + 4 - hops[q], 4)

    def forward(ch, q, i):
        send(ch.sem + 16 + q, ch.g.at[core, i], ch.g.at[core, i], partner)

    def stage_h(ch):
        for q in (1, 2, 0):
            recv(ch.sem + 10 + q, ch.g.at[core, xi, source(zi, q)], zdev[q])
        for q in range(3):
            block = ch.g.at[core, xi]
            send(ch.sem + 13 + q, block, block, xdev[q])
        forward(ch, 3, xi)

    def stage_i(ch):
        for q in (1, 2, 0):
            recv(ch.sem + 13 + q, ch.g.at[core, source(xi, q)], xdev[q])
            forward(ch, q, source(xi, q))

    def stage_j(ch):
        for q in (3, 1, 2, 0):
            i = xi if q == 3 else source(xi, q)
            recv(ch.sem + 16 + q, ch.g.at[1 - core, i], partner)

    begun = set()

    def add(f, r, n, value):
        d = s["d"][f]
        d[r:r + n] = d[r:r + n] + value if f in begun else value

    def stage_prior():
        g = chunks[0].g
        for f in factors:
            load_wait("e", f)
            pair = g[f // 2, (f % 2) * 2:(f % 2) * 2 + 2].reshape(rows_c, -1)
            row = lax.broadcasted_iota(jnp.int32, pair.shape, 0) + ctx * rows_c
            col = lax.broadcasted_iota(jnp.int32, pair.shape, 1)
            eig = jnp.sum(jnp.where(row == col, ev[f][...], 0.0), axis=1, keepdims=True)
            weighted = pair * (0.9 * eig)
            high = weighted.astype(jnp.bfloat16)
            low = (weighted - high.astype(jnp.float32)).astype(jnp.bfloat16)
            wp = s["wp"]
            wp[0] = jnp.zeros_like(wp[0])
            wp[1] = jnp.zeros_like(wp[1])
            wp[0, mine] = high
            wp[1, mine] = low
            rows = s["d"][f].shape[0]
            for r in range(0, rows, 256):
                n = min(256, rows - r)
                b = bv[f][r:r + n]
                add(f, r, n, jnp.dot(b, wp[0], preferred_element_type=jnp.float32)
                    + jnp.dot(b, wp[1], preferred_element_type=jnp.float32))
            begun.add(f)

    def stage_t(f):
        if turned[f]:
            return
        load_wait("x", f, 0)
        load_wait("x", f, 1)
        rows = xv[f].shape[1]

        @pl.loop(0, tokens // 256)
        def _(t):
            cols = pl.ds(pl.multiple_of(t * 256, 256), 256)
            for r in range(0, rows, 256):
                n = min(256, rows - r)
                s["xt"][f][r:r + n, cols] = xv[f][cols, r:r + n].T

    def stage_k(ch):
        f, d = ch.f, s["d"][ch.f]
        xt = xv[f] if turned[f] else s["xt"][f]
        rows, h = d.shape[0], 4 * ch.xb
        z = [ch.g[c].reshape(h, -1) for c in (0, 1)]
        for r in range(0, rows, 256):
            n = min(256, rows - r)
            value = [jnp.dot(xt[r:r + n, c * half + ch.t0:c * half + ch.t0 + h], z[c],
                             preferred_element_type=jnp.float32) for c in (0, 1)]
            add(f, r, n, (0.1 / total) * (value[0] + value[1]))
        begun.add(f)
        if not ch.last:
            return
        dp, fb = s["dp"][f], rows // 4
        for i in range(4):
            dp[i, 0:fb] = d[i * fb:(i + 1) * fb]
        yx, yr = s["yx"][f], s["yr"][f]
        for q, i in enumerate(around(ctx)):
            encode(dp.at[i], yx.at[q])
            send(ch.sem + 20 + q, yx.at[q], yr.at[q], ydev[q])

    def stage_m(ch):
        if not ch.last:
            return
        f = ch.f
        for q in (1, 2, 0):
            recv(ch.sem + 20 + q, s["yr"][f].at[q], ydev[q])
        n = outs[f].shape[0]
        yr = s["yr"][f]
        v = s["dp"][f][ctx]
        for p in range(3):
            v = v + decode(yr.at[p], 0, v.shape[0])
        outs[f][...] = v[0:n]

    def entry():
        for f in factors:
            dp = s["dp"][f]
            if dp.shape[1] != outs[f].shape[0]:
                dp[...] = jnp.zeros_like(dp)
        pl.semaphore_wait(barrier, len(peers))

    stages = {"a": stage_a, "d": stage_d, "f": stage_f, "h": stage_h, "i": stage_i, "j": stage_j, "k": stage_k}
    for step in SCHEDULE:
        name, k = step[0], int(step[1:])
        if name == "p" and k == 0:
            stage_core()
        elif name == "p":
            stage_probe(chunks[k], entry if k == 1 else None)
        elif name == "t":
            stage_t(k)
        elif name == "w":
            stage_prior()
        else:
            stages[name](chunks[k])
    for ch in chunks[1:]:
        stage_m(ch)

    for copy in pending:
        copy.wait_send()


def sketch(total, xs, ws, bs, es):
    tokens = xs[0].shape[0]
    r = ws[0].shape[1]
    f32, bf16 = jnp.float32, jnp.bfloat16
    vm = pltpu.VMEM

    def chunk(h, dtype, first):
        xb, zb = h // 4, h // 16
        def message(n):
            return vm((3, n, r), f32) if first else vm((3, n + SCALE_ROWS, r), bf16)
        c = dict(
            own=vm((4, xb, r), f32), cr=vm((4, xb, r), f32), zs=vm((4, zb, r), f32),
            xr=message(xb), zr=message(zb), g=vm((2, 4, 4, zb, r), dtype),
        )
        if not first:
            c["cs"] = vm((4, xb, r), f32)
            c["xs"], c["zx"] = message(xb), message(zb)
        return c

    fs = [x.shape[1] for x in xs]
    turned = [f % 128 != 0 for f in fs]
    xs = [x.T if turn else x for x, turn in zip(xs, turned)]
    fb = [-(-(f // 4) // 8) * 8 for f in fs]
    message_rows = [-(-n // 16) * 16 + SCALE_ROWS for n in fb]
    pieces = [n for _, n in PLAN for _ in range(n)]
    count = SEMS * (1 + len(pieces))
    scratch = dict(
        chunks=[chunk(r // 2, f32, True)] + [chunk(tokens // 2 // n, bf16, False) for n in pieces],
        xv=[vm(x.shape, bf16) for x in xs], wv=[vm((f, r), bf16) for f in fs],
        bv=[vm((f, r), bf16) for f in fs], ev=[vm((1, r), f32) for f in fs],
        xt=[vm((8, 128) if turn else (f, tokens), bf16) for f, turn in zip(fs, turned)],
        d=[vm((f, r), f32) for f in fs],
        dp=[vm((4, n, r), f32) for n in fb], yr=[vm((3, n, r), bf16) for n in message_rows],
        yx=[vm((3, n, r), bf16) for n in message_rows],
        cfull=vm((r, r), f32), cpart=vm((2, 4, r // 8, r), f32), wp=vm((2, r, r), bf16),
        ssem=pltpu.SemaphoreType.DMA((count,)), rsem=pltpu.SemaphoreType.DMA((count,)),
        lsem=pltpu.SemaphoreType.DMA((15,)),
    )

    def body(*refs):
        sketch_kernel(total, tokens, turned, *refs)

    return pl.pallas_call(
        body,
        out_shape=[jax.ShapeDtypeStruct((f // 4, r), f32) for f in fs],
        in_specs=[pl.BlockSpec(memory_space=pltpu.HBM)] * 12,
        out_specs=[pl.BlockSpec(memory_space=pltpu.VMEM)] * 3,
        scratch_shapes=(scratch,),
        compiler_params=pltpu.CompilerParams(
            collective_id=0, has_side_effects=True, vmem_limit_bytes=60 * 2**20),
        name="sketch",
    )(*xs, *ws, *bs, *[e.reshape(1, r) for e in es])


def place(*values):
    def body(*refs):
        for src, dst in zip(refs[:3], refs[3:]):
            dst[...] = src[...]

    return pl.pallas_call(
        body,
        out_shape=tuple(jax.ShapeDtypeStruct(v.shape, v.dtype) for v in values),
        compiler_params=pltpu.CompilerParams(vmem_limit_bytes=2 * 2**20),
        name="place",
    )(*values)


def solution(mesh):
    def per_device(*args):
        total = args[0].shape[0] * mesh.shape["context"]
        return place(*sketch(total, args[0:3], args[3:6], args[6:9], args[9:12]))

    rows = P(("section", "owner"), None)
    return jax.shard_map(
        per_device,
        mesh=mesh,
        in_specs=(P(("section", "context"), "owner"),) * 3 + (rows,) * 6 + (P("section"),) * 3,
        out_specs=(P(("section", "owner", "context"), None),) * 3,
        check_vma=False,
    )
```

```python
import jax
import jax.numpy as jnp
from jax import lax
from jax.experimental import pallas as pl
from jax.experimental.pallas import tpu as pltpu
from jax.sharding import PartitionSpec as P

PLAN = ((2, 4, 0), (2, 4, 0), (0, 4, 0), (0, 4, 0), (1, 4, 0), (1, 2, 0), (1, 2, 1))
SEMS = 32
SCHEDULE = [
    "p1", "p0", "s0", "s1", "p2", "s2", "p3", "s3", "a0", "p4", "s4", "a1", "p5", "s5",
    "a2", "p6", "s6", "a3", "p7", "s7", "t0", "a4", "a5", "d0", "t1", "a6", "a7", "d1",
    "d2", "f0", "d3", "d7", "d4", "f1", "g0", "f2", "d5", "h0", "d6", "f3", "f7", "f4",
    "g1", "i0", "h1", "g2", "j0", "w0", "h2", "g7", "h7", "f5", "f6", "g3", "i1", "h3",
    "j1", "i2", "g4", "k1", "h4", "j2", "k2", "i3", "g5", "i7", "g6", "h5", "h6", "i4",
    "j3", "k3", "j7", "k7", "j4", "k4", "i5", "i6", "j5", "k5", "j6", "k6",
]
SPAN = 86.0
SCALE_ROWS = 8


def encode(src, dst):
    rows = src.shape[0]
    tiles = [(r, min(r + 64, rows)) for r in range(0, rows, 64)]
    top = None
    for lo, hi in tiles:
        peak = jnp.max(jnp.abs(src[lo:hi]), axis=0, keepdims=True)
        top = peak if top is None else jnp.maximum(top, peak)
    scale = (top * 1.01 + 1e-30).astype(jnp.bfloat16)
    base = dst.shape[0] - SCALE_ROWS
    dst[base:base + SCALE_ROWS] = jnp.broadcast_to(scale, (SCALE_ROWS, src.shape[1]))
    slope = (2.0 * SPAN) / dst[base:base + SCALE_ROWS].astype(jnp.float32)[0:1]
    for lo, hi in tiles:
        v = src[lo:hi]
        y = jnp.exp(jnp.abs(v) * slope - SPAN)
        dst[lo:hi] = jnp.where(v < 0, -y, y).astype(jnp.bfloat16)


def decode(src, r, n):
    base = src.shape[0] - SCALE_ROWS
    slope = src[base:base + SCALE_ROWS].astype(jnp.float32)[0:1] * (0.5 / SPAN)
    y = src[pl.ds(r, n)].astype(jnp.float32)
    v = (jnp.log(jnp.abs(y)) + SPAN) * slope
    return jnp.where(y < 0, -v, v)


def sketch_kernel(total, tokens, turned, *refs):
    xs, ws, bs, es, outs = refs[0:3], refs[3:6], refs[6:9], refs[9:12], refs[12:15]
    s = refs[15]
    ssem, rsem, lsem = s["ssem"], s["rsem"], s["lsem"]
    owner, ctx = lax.axis_index("owner"), lax.axis_index("context")
    core, zi, xi = lax.rem(owner, 2), lax.rem(lax.div(owner, 2), 4), lax.div(owner, 8)

    def at(x, z, c):
        return {"owner": (lax.rem(x, 4) * 4 + lax.rem(z, 4)) * 2 + c}

    partner = at(xi, zi, 1 - core)
    hops = (2, 1, 3)
    xdev = [at(xi + h, zi, core) for h in hops]
    zdev = [at(xi, zi + h, core) for h in hops]
    ydev = [{"context": lax.rem(ctx + h, 4)} for h in hops]

    pending = []

    def remote(i, src, dst, dev):
        return pltpu.make_async_remote_copy(
            src_ref=src, dst_ref=dst, send_sem=ssem.at[i], recv_sem=rsem.at[i],
            device_id=dev, device_id_type=pl.DeviceIdType.MESH,
        )

    def send(i, src, dst, dev):
        copy = remote(i, src, dst, dev)
        copy.start()
        pending.append(copy)

    def recv(i, dst, dev):
        remote(i, dst, dst, dev).wait_recv()

    half = tokens // 2
    xv, wv, bv, ev = s["xv"], s["wv"], s["bv"], s["ev"]
    factors = list(dict.fromkeys(f for f, _, _ in PLAN))
    loads = {}
    for f in factors:
        loads["w", f] = pltpu.make_async_copy(ws[f], wv[f], lsem.at[f])
        for q, c in enumerate((1 - core, core)):
            rows = pl.ds(pl.multiple_of(c * half, half), half)
            where = (slice(None), rows) if turned[f] else rows
            loads["x", f, q] = pltpu.make_async_copy(
                xs[f].at[where], xv[f].at[where], lsem.at[3 + 2 * f + q])
        loads["b", f] = pltpu.make_async_copy(bs[f], bv[f], lsem.at[9 + f])
        loads["e", f] = pltpu.make_async_copy(es[f], ev[f], lsem.at[12 + f])
    first = factors[0]
    order = [("w", first), ("x", first, 0), ("x", first, 1)]
    order += [("w", f) for f in factors[1:]] + [("b", f) for f in factors]
    order += [("x", f, q) for f in factors[1:] for q in (0, 1)] + [("e", f) for f in factors]
    for part in order:
        loads[part].start()

    barrier = pltpu.get_barrier_semaphore()
    peers = [partner] + xdev + zdev + ydev
    for dev in peers:
        pl.semaphore_signal(barrier, inc=1, device_id=dev, device_id_type=pl.DeviceIdType.MESH)

    waited = set()

    def load_wait(*part):
        if part not in waited:
            waited.add(part)
            loads[part].wait()

    def around(i):
        return [lax.rem(i + h, 4) for h in hops]

    class Chunk:
        pass

    chunks = []
    for k, c in enumerate(s["chunks"]):
        ch = Chunk()
        ch.k, ch.sem = k, k * SEMS
        for name, ref in c.items():
            setattr(ch, name, ref)
        ch.xb, ch.zb = ch.own.shape[1], ch.g.shape[3]
        chunks.append(ch)
    taken = dict.fromkeys(factors, 0)
    for ch, (f, n, first_ring) in zip(chunks, ((None, 0, 0),) + PLAN):
        x_ring, z_ring = (xi, xdev), (zi, zdev)
        (ch.i1, ch.d1), (ch.i2, ch.d2) = (z_ring, x_ring) if first_ring else (x_ring, z_ring)
        if f is not None:
            ch.f, ch.t0 = f, taken[f] * half // 8
            taken[f] += n
    last = {chunks[int(step[1:])].f: int(step[1:]) for step in SCHEDULE if step[0] == "k"}
    for ch in chunks[1:]:
        ch.last = last[ch.f] == ch.k

    rows_c = bv[0].shape[1] // 4
    mine = pl.ds(pl.multiple_of(ctx * rows_c, rows_c), rows_c)

    def stage_core():
        ch = chunks[0]
        part = s["cpart"]
        for f in factors:
            load_wait("w", f)
            load_wait("b", f)
            s["cfull"][...] = lax.dot_general(
                bv[f][...], wv[f][...], (((0,), (0,)), ((), ())), preferred_element_type=jnp.float32)
            part[f // 2, (f % 2) * 2:(f % 2) * 2 + 2] = s["cfull"][mine].reshape(2, ch.xb, -1)
        part[1, 2:4] = jnp.zeros_like(part[1, 2:4])
        for i in range(4):
            ch.own[i] = part[core, i]

    def tile_probe(f, row, dst):
        rows = dst.shape[0]
        where = pl.ds(pl.multiple_of(row, rows), rows)
        if turned[f]:
            dst[...] = lax.dot_general(
                xv[f][:, where], wv[f][...], (((0,), (0,)), ((), ())),
                preferred_element_type=jnp.float32)
        else:
            dst[...] = jnp.dot(xv[f][where], wv[f][...], preferred_element_type=jnp.float32)

    def stage_probe(ch):
        load_wait("w", ch.f)
        for q, c, blocks in ((0, 1 - core, ch.cs), (1, core, ch.own)):
            load_wait("x", ch.f, q)
            for i in range(4):
                tile_probe(ch.f, c * half + ch.t0 + i * ch.xb, blocks.at[i])

    entered = []

    def stage_s(ch):
        if not entered:
            entered.append(entry())
        for q, i in enumerate(around(ch.i1) + [ch.i1]):
            src = s["cpart"].at[1 - core, i] if ch.k == 0 else ch.cs.at[i]
            send(ch.sem + q, src, ch.cr.at[i], partner)

    def stage_a(ch):
        for q, i in enumerate(around(ch.i1) + [ch.i1]):
            recv(ch.sem + q, ch.cr.at[i], partner)
            ch.own[i] = ch.own[i] + ch.cr[i]
            if q < 3:
                src = ch.own.at[i]
                if ch.k:
                    encode(src, ch.xs.at[q])
                    src = ch.xs.at[q]
                send(ch.sem + 4 + q, src, ch.xr.at[q], ch.d1[q])

    def stage_d(ch):
        for q in (1, 2, 0):
            recv(ch.sem + 4 + q, ch.xr.at[q], ch.d1[q])
        for q, i in enumerate(around(ch.i2) + [ch.i2]):
            r = pl.multiple_of(i * ch.zb, ch.zb)
            rows = pl.ds(r, ch.zb)
            v = ch.own[ch.i1, rows]
            for p in range(3):
                v = v + (ch.xr[p, rows] if ch.k == 0 else decode(ch.xr.at[p], r, ch.zb))
            ch.zs[i] = v
            if q < 3:
                src = ch.zs.at[i]
                if ch.k:
                    encode(src, ch.zx.at[q])
                    src = ch.zx.at[q]
                send(ch.sem + 7 + q, src, ch.zr.at[q], ch.d2[q])

    def source(i, q):
        return lax.rem(i + 4 - hops[q], 4)

    def pass_on(ch, p, i):
        block = ch.g.at[core, ch.i1, i]
        for q in range(3):
            send(ch.sem + 13 + 3 * p + q, block, block, ch.d1[q])

    def stage_f(ch):
        for q in (1, 2, 0):
            recv(ch.sem + 7 + q, ch.zr.at[q], ch.d2[q])
        v = ch.zs[ch.i2]
        for p in range(3):
            v = v + (ch.zr[p] if ch.k == 0 else decode(ch.zr.at[p], 0, ch.zb))
        ch.g[core, ch.i1, ch.i2] = v.astype(ch.g.dtype)
        for q in range(3):
            block = ch.g.at[core, ch.i1, ch.i2]
            send(ch.sem + 10 + q, block, block, ch.d2[q])
        pass_on(ch, 0, ch.i2)

    def forward(ch, q, i):
        send(ch.sem + 25 + q, ch.g.at[core, i], ch.g.at[core, i], partner)

    def arrive(ch, q, p):
        i = source(ch.i2, q)
        recv(ch.sem + 10 + q, ch.g.at[core, ch.i1, i], ch.d2[q])
        pass_on(ch, p, i)

    def stage_g(ch):
        arrive(ch, 1, 1)
        arrive(ch, 2, 2)

    def stage_h(ch):
        arrive(ch, 0, 3)
        forward(ch, 3, ch.i1)

    def stage_i(ch):
        second = [ch.i2, source(ch.i2, 1), source(ch.i2, 2), source(ch.i2, 0)]
        for q in (1, 2, 0):
            i = source(ch.i1, q)
            for p in range(4):
                recv(ch.sem + 13 + 3 * p + q, ch.g.at[core, i, second[p]], ch.d1[q])
            forward(ch, q, i)

    def stage_j(ch):
        for q in (3, 1, 2, 0):
            i = ch.i1 if q == 3 else source(ch.i1, q)
            recv(ch.sem + 25 + q, ch.g.at[1 - core, i], partner)

    begun = set()

    def add(f, r, n, value):
        d = s["d"][f]
        d[r:r + n] = d[r:r + n] + value if f in begun else value

    def stage_prior():
        g = chunks[0].g
        for f in factors:
            load_wait("e", f)
            pair = g[f // 2, (f % 2) * 2:(f % 2) * 2 + 2].reshape(rows_c, -1)
            row = lax.broadcasted_iota(jnp.int32, pair.shape, 0) + ctx * rows_c
            col = lax.broadcasted_iota(jnp.int32, pair.shape, 1)
            eig = jnp.sum(jnp.where(row == col, ev[f][...], 0.0), axis=1, keepdims=True)
            weighted = pair * (0.9 * eig)
            high = weighted.astype(jnp.bfloat16)
            low = (weighted - high.astype(jnp.float32)).astype(jnp.bfloat16)
            wp = s["wp"]
            wp[0] = jnp.zeros_like(wp[0])
            wp[1] = jnp.zeros_like(wp[1])
            wp[0, mine] = high
            wp[1, mine] = low
            rows = s["d"][f].shape[0]
            for r in range(0, rows, 256):
                n = min(256, rows - r)
                b = bv[f][r:r + n]
                add(f, r, n, jnp.dot(b, wp[0], preferred_element_type=jnp.float32)
                    + jnp.dot(b, wp[1], preferred_element_type=jnp.float32))
            begun.add(f)

    def stage_t(f):
        if turned[f]:
            return
        load_wait("x", f, 0)
        load_wait("x", f, 1)
        rows = xv[f].shape[1]

        @pl.loop(0, tokens // 256)
        def _(t):
            cols = pl.ds(pl.multiple_of(t * 256, 256), 256)
            for r in range(0, rows, 256):
                n = min(256, rows - r)
                s["xt"][f][r:r + n, cols] = xv[f][cols, r:r + n].T

    def stage_k(ch):
        f, d = ch.f, s["d"][ch.f]
        xt = xv[f] if turned[f] else s["xt"][f]
        rows, h = d.shape[0], 4 * ch.xb
        z = [ch.g[c].reshape(h, -1) for c in (0, 1)]
        for r in range(0, rows, 256):
            n = min(256, rows - r)
            value = [jnp.dot(xt[r:r + n, c * half + ch.t0:c * half + ch.t0 + h], z[c],
                             preferred_element_type=jnp.float32) for c in (0, 1)]
            add(f, r, n, (0.1 / total) * (value[0] + value[1]))
        begun.add(f)
        if not ch.last:
            return
        dp, fb = s["dp"][f], rows // 4
        for i in range(4):
            dp[i, 0:fb] = d[i * fb:(i + 1) * fb]
        yx, yr = s["yx"][f], s["yr"][f]
        for q, i in enumerate(around(ctx)):
            encode(dp.at[i], yx.at[q])
            send(ch.sem + 29 + q, yx.at[q], yr.at[q], ydev[q])

    def stage_m(ch):
        if not ch.last:
            return
        f = ch.f
        for q in (1, 2, 0):
            recv(ch.sem + 29 + q, s["yr"][f].at[q], ydev[q])
        n = outs[f].shape[0]
        yr = s["yr"][f]
        v = s["dp"][f][ctx]
        for p in range(3):
            v = v + decode(yr.at[p], 0, v.shape[0])
        outs[f][...] = v[0:n]

    def entry():
        for f in factors:
            dp = s["dp"][f]
            if dp.shape[1] != outs[f].shape[0]:
                dp[...] = jnp.zeros_like(dp)
        pl.semaphore_wait(barrier, len(peers))

    stages = {"s": stage_s, "a": stage_a, "d": stage_d, "f": stage_f, "g": stage_g, "h": stage_h,
              "i": stage_i, "j": stage_j, "k": stage_k}
    for step in SCHEDULE:
        name, k = step[0], int(step[1:])
        if name == "p" and k == 0:
            stage_core()
        elif name == "p":
            stage_probe(chunks[k])
        elif name == "t":
            stage_t(k)
        elif name == "w":
            stage_prior()
        else:
            stages[name](chunks[k])
    for ch in chunks[1:]:
        stage_m(ch)

    for copy in pending:
        copy.wait_send()


def sketch(total, xs, ws, bs, es):
    tokens = xs[0].shape[0]
    r = ws[0].shape[1]
    f32, bf16 = jnp.float32, jnp.bfloat16
    vm = pltpu.VMEM

    def chunk(h, dtype, first):
        xb, zb = h // 4, h // 16
        def message(n):
            return vm((3, n, r), f32) if first else vm((3, n + SCALE_ROWS, r), bf16)
        c = dict(
            own=vm((4, xb, r), f32), cr=vm((4, xb, r), f32), zs=vm((4, zb, r), f32),
            xr=message(xb), zr=message(zb), g=vm((2, 4, 4, zb, r), dtype),
        )
        if not first:
            c["cs"] = vm((4, xb, r), f32)
            c["xs"], c["zx"] = message(xb), message(zb)
        return c

    fs = [x.shape[1] for x in xs]
    turned = [f % 128 != 0 for f in fs]
    xs = [x.T if turn else x for x, turn in zip(xs, turned)]
    fb = [-(-(f // 4) // 8) * 8 for f in fs]
    message_rows = [-(-n // 16) * 16 + SCALE_ROWS for n in fb]
    pieces = [n for _, n, _ in PLAN]
    count = SEMS * (1 + len(pieces))
    scratch = dict(
        chunks=[chunk(r // 2, f32, True)] + [chunk(tokens * n // 16, bf16, False) for n in pieces],
        xv=[vm(x.shape, bf16) for x in xs], wv=[vm((f, r), bf16) for f in fs],
        bv=[vm((f, r), bf16) for f in fs], ev=[vm((1, r), f32) for f in fs],
        xt=[vm((8, 128) if turn else (f, tokens), bf16) for f, turn in zip(fs, turned)],
        d=[vm((f, r), f32) for f in fs],
        dp=[vm((4, n, r), f32) for n in fb], yr=[vm((3, n, r), bf16) for n in message_rows],
        yx=[vm((3, n, r), bf16) for n in message_rows],
        cfull=vm((r, r), f32), cpart=vm((2, 4, r // 8, r), f32), wp=vm((2, r, r), bf16),
        ssem=pltpu.SemaphoreType.DMA((count,)), rsem=pltpu.SemaphoreType.DMA((count,)),
        lsem=pltpu.SemaphoreType.DMA((15,)),
    )

    def body(*refs):
        sketch_kernel(total, tokens, turned, *refs)

    return pl.pallas_call(
        body,
        out_shape=[jax.ShapeDtypeStruct((f // 4, r), f32) for f in fs],
        in_specs=[pl.BlockSpec(memory_space=pltpu.HBM)] * 12,
        out_specs=[pl.BlockSpec(memory_space=pltpu.VMEM)] * 3,
        scratch_shapes=(scratch,),
        compiler_params=pltpu.CompilerParams(
            collective_id=0, has_side_effects=True, vmem_limit_bytes=60 * 2**20),
        name="sketch",
    )(*xs, *ws, *bs, *[e.reshape(1, r) for e in es])


def place(*values):
    def body(*refs):
        for src, dst in zip(refs[:3], refs[3:]):
            dst[...] = src[...]

    return pl.pallas_call(
        body,
        out_shape=tuple(jax.ShapeDtypeStruct(v.shape, v.dtype) for v in values),
        compiler_params=pltpu.CompilerParams(vmem_limit_bytes=60 * 2**20),
        name="place",
    )(*values)


def solution(mesh):
    def per_device(*args):
        total = args[0].shape[0] * mesh.shape["context"]
        return place(*sketch(total, args[0:3], args[3:6], args[6:9], args[9:12]))

    rows = P(("section", "owner"), None)
    return jax.shard_map(
        per_device,
        mesh=mesh,
        in_specs=(P(("section", "context"), "owner"),) * 3 + (rows,) * 6 + (P("section"),) * 3,
        out_specs=(P(("section", "owner", "context"), None),) * 3,
        check_vma=False,
    )
```

```python
import jax
import jax.numpy as jnp
from jax import lax
from jax.experimental import pallas as pl
from jax.experimental.pallas import tpu as pltpu
from jax.sharding import PartitionSpec as P

PLAN = ((2, 4, 0), (2, 4, 0), (0, 4, 0), (0, 4, 0), (1, 4, 0), (1, 2, 0), (1, 2, 1))
SEMS = 32
SCHEDULE = [
    "p1", "p0", "s0", "s1", "p2", "s2", "p3", "s3", "a0", "p4", "s4", "a1", "p5", "s5",
    "a2", "p6", "s6", "a3", "p7", "s7", "t0", "a4", "a5", "d0", "t1", "a6", "a7", "d1",
    "d2", "f0", "d3", "d7", "d4", "f1", "g0", "f2", "d5", "h0", "d6", "f3", "f7", "f4",
    "g1", "i0", "h1", "g2", "j0", "w0", "h2", "g7", "h7", "f5", "f6", "g3", "i1", "h3",
    "j1", "i2", "g4", "k1", "h4", "j2", "k2", "i3", "g5", "i7", "g6", "h5", "h6", "i4",
    "j3", "k3", "j7", "k7", "j4", "k4", "i5", "i6", "j5", "k5", "j6", "k6",
]
SPAN = 86.0
SCALE_ROWS = 8


def encode(src, dst):
    rows = src.shape[0]
    tiles = [(r, min(r + 64, rows)) for r in range(0, rows, 64)]
    top = None
    for lo, hi in tiles:
        peak = jnp.max(jnp.abs(src[lo:hi]), axis=0, keepdims=True)
        top = peak if top is None else jnp.maximum(top, peak)
    scale = (top * 1.01 + 1e-30).astype(jnp.bfloat16)
    base = dst.shape[0] - SCALE_ROWS
    dst[base:base + SCALE_ROWS] = jnp.broadcast_to(scale, (SCALE_ROWS, src.shape[1]))
    slope = (2.0 * SPAN) / dst[base:base + SCALE_ROWS].astype(jnp.float32)[0:1]
    for lo, hi in tiles:
        v = src[lo:hi]
        y = jnp.exp(jnp.abs(v) * slope - SPAN)
        dst[lo:hi] = jnp.where(v < 0, -y, y).astype(jnp.bfloat16)


def decode(src, r, n):
    base = src.shape[0] - SCALE_ROWS
    slope = src[base:base + SCALE_ROWS].astype(jnp.float32)[0:1] * (0.5 / SPAN)
    y = src[pl.ds(r, n)].astype(jnp.float32)
    v = (jnp.log(jnp.abs(y)) + SPAN) * slope
    return jnp.where(y < 0, -v, v)


def sketch_kernel(total, tokens, turned, *refs):
    xs, ws, bs, es, outs = refs[0:3], refs[3:6], refs[6:9], refs[9:12], refs[12:15]
    s = refs[15]
    ssem, rsem, lsem = s["ssem"], s["rsem"], s["lsem"]
    owner, ctx = lax.axis_index("owner"), lax.axis_index("context")
    core, zi, xi = lax.rem(owner, 2), lax.rem(lax.div(owner, 2), 4), lax.div(owner, 8)

    def at(x, z, c):
        return {"owner": (lax.rem(x, 4) * 4 + lax.rem(z, 4)) * 2 + c}

    partner = at(xi, zi, 1 - core)
    hops = (2, 1, 3)
    xdev = [at(xi + h, zi, core) for h in hops]
    zdev = [at(xi, zi + h, core) for h in hops]
    ydev = [{"context": lax.rem(ctx + h, 4)} for h in hops]

    pending = []

    def remote(i, src, dst, dev):
        return pltpu.make_async_remote_copy(
            src_ref=src, dst_ref=dst, send_sem=ssem.at[i], recv_sem=rsem.at[i],
            device_id=dev, device_id_type=pl.DeviceIdType.MESH,
        )

    def send(i, src, dst, dev):
        copy = remote(i, src, dst, dev)
        copy.start()
        pending.append(copy)

    def recv(i, dst, dev):
        remote(i, dst, dst, dev).wait_recv()

    half = tokens // 2
    xv, wv, bv, ev = s["xv"], s["wv"], s["bv"], s["ev"]
    factors = list(dict.fromkeys(f for f, _, _ in PLAN))
    loads = {}
    begin, pieces = dict.fromkeys(factors, 0), []
    for k, (f, n, _) in enumerate(PLAN):
        for q, c in enumerate((1 - core, core)):
            size = n * half // 8
            rows = pl.ds(pl.multiple_of(c * half + begin[f], size), size)
            where = (slice(None), rows) if turned[f] else rows
            pieces.append(("x", f, q, begin[f]))
            loads[pieces[-1]] = pltpu.make_async_copy(
                xs[f].at[where], xv[f].at[where], lsem.at[9 + 2 * k + q])
        begin[f] += n * half // 8
    for f in factors:
        loads["w", f] = pltpu.make_async_copy(ws[f], wv[f], lsem.at[f])
        loads["b", f] = pltpu.make_async_copy(bs[f], bv[f], lsem.at[3 + f])
        loads["e", f] = pltpu.make_async_copy(es[f], ev[f], lsem.at[6 + f])
    first = factors[0]
    order = [("w", first)] + pieces[:2]
    order += [("w", f) for f in factors[1:]] + [("b", f) for f in factors]
    order += pieces[2:] + [("e", f) for f in factors]
    for part in order:
        loads[part].start()

    barrier = pltpu.get_barrier_semaphore()
    peers = [partner] + xdev + zdev + ydev
    for dev in peers:
        pl.semaphore_signal(barrier, inc=1, device_id=dev, device_id_type=pl.DeviceIdType.MESH)

    waited = set()

    def load_wait(*part):
        if part not in waited:
            waited.add(part)
            loads[part].wait()

    def around(i):
        return [lax.rem(i + h, 4) for h in hops]

    class Chunk:
        pass

    chunks = []
    for k, c in enumerate(s["chunks"]):
        ch = Chunk()
        ch.k, ch.sem = k, k * SEMS
        for name, ref in c.items():
            setattr(ch, name, ref)
        ch.xb, ch.zb = ch.own.shape[1], ch.g.shape[3]
        chunks.append(ch)
    taken = dict.fromkeys(factors, 0)
    for ch, (f, n, first_ring) in zip(chunks, ((None, 0, 0),) + PLAN):
        x_ring, z_ring = (xi, xdev), (zi, zdev)
        (ch.i1, ch.d1), (ch.i2, ch.d2) = (z_ring, x_ring) if first_ring else (x_ring, z_ring)
        if f is not None:
            ch.f, ch.t0 = f, taken[f] * half // 8
            taken[f] += n
    last = {chunks[int(step[1:])].f: int(step[1:]) for step in SCHEDULE if step[0] == "k"}
    for ch in chunks[1:]:
        ch.last = last[ch.f] == ch.k

    rows_c = bv[0].shape[1] // 4
    mine = pl.ds(pl.multiple_of(ctx * rows_c, rows_c), rows_c)

    def stage_core():
        ch = chunks[0]
        part = s["cpart"]
        for f in factors:
            load_wait("w", f)
            load_wait("b", f)
            s["cfull"][...] = lax.dot_general(
                bv[f][...], wv[f][...], (((0,), (0,)), ((), ())), preferred_element_type=jnp.float32)
            part[f // 2, (f % 2) * 2:(f % 2) * 2 + 2] = s["cfull"][mine].reshape(2, ch.xb, -1)
        part[1, 2:4] = jnp.zeros_like(part[1, 2:4])
        for i in range(4):
            ch.own[i] = part[core, i]

    def tile_probe(f, row, dst):
        rows = dst.shape[0]
        where = pl.ds(pl.multiple_of(row, rows), rows)
        if turned[f]:
            dst[...] = lax.dot_general(
                xv[f][:, where], wv[f][...], (((0,), (0,)), ((), ())),
                preferred_element_type=jnp.float32)
        else:
            dst[...] = jnp.dot(xv[f][where], wv[f][...], preferred_element_type=jnp.float32)

    def stage_probe(ch):
        load_wait("w", ch.f)
        for q, c, blocks in ((0, 1 - core, ch.cs), (1, core, ch.own)):
            load_wait("x", ch.f, q, ch.t0)
            for i in range(4):
                tile_probe(ch.f, c * half + ch.t0 + i * ch.xb, blocks.at[i])

    entered = []

    def stage_s(ch):
        if not entered:
            entered.append(entry())
        for q, i in enumerate(around(ch.i1) + [ch.i1]):
            src = s["cpart"].at[1 - core, i] if ch.k == 0 else ch.cs.at[i]
            send(ch.sem + q, src, ch.cr.at[i], partner)

    def stage_a(ch):
        for q, i in enumerate(around(ch.i1) + [ch.i1]):
            recv(ch.sem + q, ch.cr.at[i], partner)
            ch.own[i] = ch.own[i] + ch.cr[i]
            if q < 3:
                src = ch.own.at[i]
                if ch.k:
                    encode(src, ch.xs.at[q])
                    src = ch.xs.at[q]
                send(ch.sem + 4 + q, src, ch.xr.at[q], ch.d1[q])

    def stage_d(ch):
        for q in (1, 2, 0):
            recv(ch.sem + 4 + q, ch.xr.at[q], ch.d1[q])
        for q, i in enumerate(around(ch.i2) + [ch.i2]):
            r = pl.multiple_of(i * ch.zb, ch.zb)
            rows = pl.ds(r, ch.zb)
            v = ch.own[ch.i1, rows]
            for p in range(3):
                v = v + (ch.xr[p, rows] if ch.k == 0 else decode(ch.xr.at[p], r, ch.zb))
            ch.zs[i] = v
            if q < 3:
                src = ch.zs.at[i]
                if ch.k:
                    encode(src, ch.zx.at[q])
                    src = ch.zx.at[q]
                send(ch.sem + 7 + q, src, ch.zr.at[q], ch.d2[q])

    def source(i, q):
        return lax.rem(i + 4 - hops[q], 4)

    def pass_on(ch, p, i):
        block = ch.g.at[core, ch.i1, i]
        for q in range(3):
            send(ch.sem + 13 + 3 * p + q, block, block, ch.d1[q])

    def stage_f(ch):
        for q in (1, 2, 0):
            recv(ch.sem + 7 + q, ch.zr.at[q], ch.d2[q])
        v = ch.zs[ch.i2]
        for p in range(3):
            v = v + (ch.zr[p] if ch.k == 0 else decode(ch.zr.at[p], 0, ch.zb))
        ch.g[core, ch.i1, ch.i2] = v.astype(ch.g.dtype)
        for q in range(3):
            block = ch.g.at[core, ch.i1, ch.i2]
            send(ch.sem + 10 + q, block, block, ch.d2[q])
        pass_on(ch, 0, ch.i2)

    def forward(ch, q, i):
        send(ch.sem + 25 + q, ch.g.at[core, i], ch.g.at[core, i], partner)

    def arrive(ch, q, p):
        i = source(ch.i2, q)
        recv(ch.sem + 10 + q, ch.g.at[core, ch.i1, i], ch.d2[q])
        pass_on(ch, p, i)

    def stage_g(ch):
        arrive(ch, 1, 1)
        arrive(ch, 2, 2)

    def stage_h(ch):
        arrive(ch, 0, 3)
        forward(ch, 3, ch.i1)

    def stage_i(ch):
        second = [ch.i2, source(ch.i2, 1), source(ch.i2, 2), source(ch.i2, 0)]
        for q in (1, 2, 0):
            i = source(ch.i1, q)
            for p in range(4):
                recv(ch.sem + 13 + 3 * p + q, ch.g.at[core, i, second[p]], ch.d1[q])
            forward(ch, q, i)

    def stage_j(ch):
        for q in (3, 1, 2, 0):
            i = ch.i1 if q == 3 else source(ch.i1, q)
            recv(ch.sem + 25 + q, ch.g.at[1 - core, i], partner)

    begun = set()

    def add(f, r, n, value):
        d = s["d"][f]
        d[r:r + n] = d[r:r + n] + value if f in begun else value

    def stage_prior():
        g = chunks[0].g
        for f in factors:
            load_wait("e", f)
            pair = g[f // 2, (f % 2) * 2:(f % 2) * 2 + 2].reshape(rows_c, -1)
            row = lax.broadcasted_iota(jnp.int32, pair.shape, 0) + ctx * rows_c
            col = lax.broadcasted_iota(jnp.int32, pair.shape, 1)
            eig = jnp.sum(jnp.where(row == col, ev[f][...], 0.0), axis=1, keepdims=True)
            weighted = pair * (0.9 * eig)
            high = weighted.astype(jnp.bfloat16)
            low = (weighted - high.astype(jnp.float32)).astype(jnp.bfloat16)
            wp = s["wp"]
            wp[0] = jnp.zeros_like(wp[0])
            wp[1] = jnp.zeros_like(wp[1])
            wp[0, mine] = high
            wp[1, mine] = low
            rows = s["d"][f].shape[0]
            for r in range(0, rows, 256):
                n = min(256, rows - r)
                b = bv[f][r:r + n]
                add(f, r, n, jnp.dot(b, wp[0], preferred_element_type=jnp.float32)
                    + jnp.dot(b, wp[1], preferred_element_type=jnp.float32))
            begun.add(f)

    def stage_t(f):
        if turned[f]:
            return
        for piece in pieces:
            if piece[1] == f:
                load_wait(*piece)
        rows = xv[f].shape[1]

        @pl.loop(0, tokens // 256)
        def _(t):
            cols = pl.ds(pl.multiple_of(t * 256, 256), 256)
            for r in range(0, rows, 256):
                n = min(256, rows - r)
                s["xt"][f][r:r + n, cols] = xv[f][cols, r:r + n].T

    def stage_k(ch):
        f, d = ch.f, s["d"][ch.f]
        xt = xv[f] if turned[f] else s["xt"][f]
        rows, h = d.shape[0], 4 * ch.xb
        z = [ch.g[c].reshape(h, -1) for c in (0, 1)]
        for r in range(0, rows, 256):
            n = min(256, rows - r)
            value = [jnp.dot(xt[r:r + n, c * half + ch.t0:c * half + ch.t0 + h], z[c],
                             preferred_element_type=jnp.float32) for c in (0, 1)]
            add(f, r, n, (0.1 / total) * (value[0] + value[1]))
        begun.add(f)
        if not ch.last:
            return
        dp, fb = s["dp"][f], rows // 4
        for i in range(4):
            dp[i, 0:fb] = d[i * fb:(i + 1) * fb]
        yx, yr = s["yx"][f], s["yr"][f]
        for q, i in enumerate(around(ctx)):
            encode(dp.at[i], yx.at[q])
            send(ch.sem + 29 + q, yx.at[q], yr.at[q], ydev[q])

    def stage_m(ch):
        if not ch.last:
            return
        f = ch.f
        for q in (1, 2, 0):
            recv(ch.sem + 29 + q, s["yr"][f].at[q], ydev[q])
        n = outs[f].shape[0]
        yr = s["yr"][f]
        v = s["dp"][f][ctx]
        for p in range(3):
            v = v + decode(yr.at[p], 0, v.shape[0])
        outs[f][...] = v[0:n]

    def entry():
        for f in factors:
            dp = s["dp"][f]
            if dp.shape[1] != outs[f].shape[0]:
                dp[...] = jnp.zeros_like(dp)
        pl.semaphore_wait(barrier, len(peers))

    stages = {"s": stage_s, "a": stage_a, "d": stage_d, "f": stage_f, "g": stage_g, "h": stage_h,
              "i": stage_i, "j": stage_j, "k": stage_k}
    for step in SCHEDULE:
        name, k = step[0], int(step[1:])
        if name == "p" and k == 0:
            stage_core()
        elif name == "p":
            stage_probe(chunks[k])
        elif name == "t":
            stage_t(k)
        elif name == "w":
            stage_prior()
        else:
            stages[name](chunks[k])
    for ch in chunks[1:]:
        stage_m(ch)

    for copy in pending:
        copy.wait_send()


def sketch(total, xs, ws, bs, es):
    tokens = xs[0].shape[0]
    r = ws[0].shape[1]
    f32, bf16 = jnp.float32, jnp.bfloat16
    vm = pltpu.VMEM

    def chunk(h, dtype, first):
        xb, zb = h // 4, h // 16
        def message(n):
            return vm((3, n, r), f32) if first else vm((3, n + SCALE_ROWS, r), bf16)
        c = dict(
            own=vm((4, xb, r), f32), cr=vm((4, xb, r), f32), zs=vm((4, zb, r), f32),
            xr=message(xb), zr=message(zb), g=vm((2, 4, 4, zb, r), dtype),
        )
        if not first:
            c["cs"] = vm((4, xb, r), f32)
            c["xs"], c["zx"] = message(xb), message(zb)
        return c

    fs = [x.shape[1] for x in xs]
    turned = [f % 128 != 0 for f in fs]
    xs = [x.T if turn else x for x, turn in zip(xs, turned)]
    fb = [-(-(f // 4) // 8) * 8 for f in fs]
    message_rows = [-(-n // 16) * 16 + SCALE_ROWS for n in fb]
    pieces = [n for _, n, _ in PLAN]
    count = SEMS * (1 + len(pieces))
    scratch = dict(
        chunks=[chunk(r // 2, f32, True)] + [chunk(tokens * n // 16, bf16, False) for n in pieces],
        xv=[vm(x.shape, bf16) for x in xs], wv=[vm((f, r), bf16) for f in fs],
        bv=[vm((f, r), bf16) for f in fs], ev=[vm((1, r), f32) for f in fs],
        xt=[vm((8, 128) if turn else (f, tokens), bf16) for f, turn in zip(fs, turned)],
        d=[vm((f, r), f32) for f in fs],
        dp=[vm((4, n, r), f32) for n in fb], yr=[vm((3, n, r), bf16) for n in message_rows],
        yx=[vm((3, n, r), bf16) for n in message_rows],
        cfull=vm((r, r), f32), cpart=vm((2, 4, r // 8, r), f32), wp=vm((2, r, r), bf16),
        ssem=pltpu.SemaphoreType.DMA((count,)), rsem=pltpu.SemaphoreType.DMA((count,)),
        lsem=pltpu.SemaphoreType.DMA((9 + 2 * len(PLAN),)),
    )

    def body(*refs):
        sketch_kernel(total, tokens, turned, *refs)

    return pl.pallas_call(
        body,
        out_shape=[jax.ShapeDtypeStruct((f // 4, r), f32) for f in fs],
        in_specs=[pl.BlockSpec(memory_space=pltpu.HBM)] * 12,
        out_specs=[pl.BlockSpec(memory_space=pltpu.VMEM)] * 3,
        scratch_shapes=(scratch,),
        compiler_params=pltpu.CompilerParams(
            collective_id=0, has_side_effects=True, vmem_limit_bytes=60 * 2**20),
        name="sketch",
    )(*xs, *ws, *bs, *[e.reshape(1, r) for e in es])


def place(*values):
    def body(*refs):
        for src, dst in zip(refs[:3], refs[3:]):
            dst[...] = src[...]

    return pl.pallas_call(
        body,
        out_shape=tuple(jax.ShapeDtypeStruct(v.shape, v.dtype) for v in values),
        compiler_params=pltpu.CompilerParams(vmem_limit_bytes=60 * 2**20),
        name="place",
    )(*values)


def solution(mesh):
    def per_device(*args):
        total = args[0].shape[0] * mesh.shape["context"]
        return place(*sketch(total, args[0:3], args[3:6], args[6:9], args[9:12]))

    rows = P(("section", "owner"), None)
    return jax.shard_map(
        per_device,
        mesh=mesh,
        in_specs=(P(("section", "context"), "owner"),) * 3 + (rows,) * 6 + (P("section"),) * 3,
        out_specs=(P(("section", "owner", "context"), None),) * 3,
        check_vma=False,
    )
```
